32 devices in a mesh: grp: 4 (over y, x), node: 8 (over z, core).
Axes of the slice: x: 2, y: 2, z: 4, core: 2. Of those that a mesh axis runs over, the one named last changes fastest.
Arguments:
- coefficients: float32 [8192, 1024], P(('grp', 'node')), may hold values from -6 to 6
- transfer: float32 [5, 8192, 512], P(None, ('grp', 'node')), may hold values from -0.3125 to 0.3125
- ranks: int32 [5, 32], P(None, ('grp', 'node')), may hold values from 128 to 256, as said below
Outputs:
- applied: float32 [8192, 1024], P(('grp', 'node'))
The draws below stay inside these ranges and needn't reach their ends.
Inputs may be any that keep to these rules, and one draw needn't show every extreme that they name: `ranks`: in each level some block has rank exactly 256 and some block rank 256 // 2.
All inputs are finite; a program needn't handle non-finite values.
Results may differ from the reference program's by a relative error of at most 0.00011.
Values sent between devices are 32-bit elements; how exact they have to be, the bound alone decides.
A program may use at most 128 MiB of HBM per device.

```python
import jax
import jax.numpy as jnp
from jax import lax

K = 256
R = 1024
LEVELS = 5
BLOCKS = 32
ORDER = 8192
N_GRP = 4
N_NODE = 8


def draw_ranks(key, part):
    values = jax.random.randint(key, (LEVELS, BLOCKS), K // 2, K + 1).astype(jnp.int32)
    top_pos = jax.random.randint(jax.random.fold_in(key, 11), (LEVELS,), 0, BLOCKS)
    low_pos = (top_pos + 1 + jax.random.randint(jax.random.fold_in(key, 12), (LEVELS,), 0, BLOCKS - 1)) % BLOCKS
    level_ids = jnp.arange(LEVELS)
    values = values.at[level_ids, top_pos].set(K)
    values = values.at[level_ids, low_pos].set(K // 2)
    return values.astype(jnp.int32)


def block_scale(rng, dims, shards, least, top_value):
    def one(dim, parts):
        draws = jax.random.uniform(jax.random.fold_in(jax.random.fold_in(rng, 6), dim), (parts,), jnp.float32, least / len(shards), top_value / len(shards))
        return jnp.repeat(jnp.exp(draws), dims[dim] // parts).reshape((-1,) + (1,) * (len(dims) - dim - 1))

    level = one(*shards[0])
    for cut in shards[1:]:
        level = level * one(*cut)
    return level


def gaussian(key, dims, spread, bound, cuts=(), kind=jnp.bfloat16):
    drawn = spread * jax.random.normal(key, dims, jnp.float32)
    if cuts:
        drawn = drawn * block_scale(key, dims, cuts, -0.22, 0.18)
    return jnp.clip(drawn, -bound, bound).astype(kind)


def setup_inputs(seed: int = 0) -> dict:
    splits = jax.random.split(jax.random.key(seed), 4)
    return {
        "coefficients": gaussian(splits[0], (ORDER, R), 1.0, 6.0, ((0, 32),), jnp.float32),
        "transfer": gaussian(splits[1], (LEVELS, ORDER, 2 * K), (K * 3 // 2) ** -0.5, 0.3125, ((1, 32),), jnp.float32),
        "ranks": draw_ranks(jax.random.fold_in(splits[3], 71), 0),
    }


def reference(coefficients, transfer, ranks):
    blocks = N_GRP * N_NODE
    current = coefficients.reshape(blocks, K, R)
    row_ids = jnp.arange(K, dtype=jnp.int32)
    for level in range(LEVELS):
        span = 2 ** level
        outer = blocks // (2 * span)
        paired = current.reshape(outer, 2, span, K, R)
        stacked = jnp.concatenate([paired[:, 0], paired[:, 1]], axis=2)
        matrices = transfer[level].reshape(outer, 2, span, K, 2 * K)
        mixed = jnp.einsum("aibkm,abmr->aibkr", matrices, stacked, precision=lax.Precision.HIGHEST)
        limits = ranks[level].reshape(outer, 2, span)
        keep = row_ids[None, None, None, :] < limits[..., None]
        current = jnp.where(keep[..., None], mixed, jnp.zeros_like(mixed)).reshape(blocks, K, R)
    return current.reshape(blocks * K, R)
```

```python
import functools

import jax
import jax.numpy as jnp
from jax import lax
from jax.experimental import pallas as pl
from jax.experimental.pallas import tpu as pltpu
from jax.sharding import PartitionSpec as P

LANES = 128


def split_cols(x):
    high = x.astype(jnp.bfloat16)
    low = (x - high.astype(jnp.float32)).astype(jnp.bfloat16)
    return high, low


def plan(node_bits, group_bits):
    levels, due = [], 0
    for bit in range(node_bits):
        if bit:
            due += 1 if bit == 1 else 2
        levels.append(("node", bit, due))
    for bit in range(group_bits):
        due += 1
        levels.append(("grp", bit, due))
    return levels


def kernel(
    levels, ranks_ref, coef_ref, transfer_ref, out_ref,
    raw, mats, own, landed, mixed, stage,
    raw_sem, stage_sem, out_sem, send_sem, recv_sem,
):
    depth = coef_ref.shape[0]
    chunks, width = landed.shape[1], landed.shape[3]
    count = len(levels)

    places, partners = [], []
    for axis, bit, _ in levels:
        place = lax.axis_index(axis)
        upper = (place // 2**bit) % 2
        places.append(upper)
        partners.append({axis: place + (1 - 2 * upper) * 2**bit})

    def cols(chunk):
        return pl.ds(pl.multiple_of(chunk * width, width), width)

    def load_chunk(chunk):
        return pltpu.make_async_copy(
            coef_ref.at[:, cols(chunk)], stage.at[chunk], stage_sem.at[chunk]
        )

    def load_matrix(level):
        return pltpu.make_async_copy(transfer_ref.at[level], raw.at[level], raw_sem.at[level])

    def store_chunk(chunk):
        return pltpu.make_async_copy(
            mixed.at[count - 1, chunk], out_ref.at[:, cols(chunk)], out_sem.at[chunk]
        )

    def send(level, chunk):
        source = coef_ref.at[:, cols(chunk)] if level == 0 else mixed.at[level - 1, chunk]
        return pltpu.make_async_remote_copy(
            src_ref=source,
            dst_ref=landed.at[level, chunk],
            send_sem=send_sem.at[level, chunk],
            recv_sem=recv_sem.at[level, chunk],
            device_id=partners[level],
            device_id_type=pl.DeviceIdType.MESH,
        )

    barrier = pltpu.get_barrier_semaphore()
    for level in range(count):
        pl.semaphore_signal(
            barrier, inc=1, device_id=partners[level], device_id_type=pl.DeviceIdType.MESH
        )
    load_matrix(0).start()
    for chunk in range(chunks):
        load_chunk(chunk).start()
    for level in range(1, count):
        load_matrix(level).start()
    pl.semaphore_wait(barrier, count)
    for chunk in range(chunks):
        send(0, chunk).start()

    rows = lax.broadcasted_iota(jnp.int32, (depth, depth), 0)
    for level in range(count):
        load_matrix(level).wait()
        keep = rows < ranks_ref[0, level]
        for half, place in enumerate((places[level], 1 - places[level])):
            block = raw[level, :, pl.ds(pl.multiple_of(place * depth, depth), depth)]
            high, low = split_cols(jnp.where(keep, block, jnp.zeros_like(block)))
            mats[level, :depth, half * depth:(half + 1) * depth] = high
            mats[level, depth:, half * depth:(half + 1) * depth] = low

    def store_own(chunk, x):
        high, low = split_cols(x)
        own[chunk, :, :width] = high
        own[chunk, :, width:] = low

    for chunk in range(chunks):
        load_chunk(chunk).wait()
        store_own(chunk, stage[chunk])

    def task(level, chunk):
        send(level, chunk).wait_recv()
        other = jnp.concatenate(split_cols(landed[level, chunk]), axis=1)
        total = jnp.dot(
            mats[level, :, :depth], own[chunk], preferred_element_type=jnp.float32
        ) + jnp.dot(mats[level, :, depth:], other, preferred_element_type=jnp.float32)
        total = total[:depth] + total[depth:]
        result = total[:, :width] + total[:, width:]
        mixed[level, chunk] = result
        if level + 1 < count:
            store_own(chunk, result)
            send(level + 1, chunk).start()
        else:
            store_chunk(chunk).start()

    def step(s, carry):
        for level, (_, _, due) in enumerate(levels):
            @pl.when((s >= due) & (s < due + chunks))
            def _():
                task(level, s - due)
        return carry

    lax.fori_loop(0, levels[-1][2] + chunks, step, 0)

    def finish(chunk, carry):
        store_chunk(chunk).wait()
        for level in range(count):
            send(level, chunk).wait_send()
        return carry

    lax.fori_loop(0, chunks, finish, 0)


def per_device(coefficients, transfer, ranks):
    levels = plan(
        lax.axis_size("node").bit_length() - 1, lax.axis_size("grp").bit_length() - 1
    )
    count = len(levels)
    depth, width = coefficients.shape
    chunks = width // LANES
    call = pl.pallas_call(
        functools.partial(kernel, levels),
        out_shape=jax.ShapeDtypeStruct(coefficients.shape, jnp.float32),
        in_specs=[
            pl.BlockSpec(memory_space=pltpu.SMEM),
            pl.BlockSpec(memory_space=pl.ANY),
            pl.BlockSpec(memory_space=pl.ANY),
        ],
        out_specs=pl.BlockSpec(memory_space=pl.ANY),
        scratch_shapes=[
            pltpu.VMEM((count, depth, 2 * depth), jnp.float32),
            pltpu.VMEM((count, 2 * depth, 2 * depth), jnp.bfloat16),
            pltpu.VMEM((chunks, depth, 2 * LANES), jnp.bfloat16),
            pltpu.VMEM((count, chunks, depth, LANES), jnp.float32),
            pltpu.VMEM((count, chunks, depth, LANES), jnp.float32),
            pltpu.VMEM((chunks, depth, LANES), jnp.float32),
            pltpu.SemaphoreType.DMA((count,)),
            pltpu.SemaphoreType.DMA((chunks,)),
            pltpu.SemaphoreType.DMA((chunks,)),
            pltpu.SemaphoreType.DMA((count, chunks)),
            pltpu.SemaphoreType.DMA((count, chunks)),
        ],
        compiler_params=pltpu.CompilerParams(collective_id=0, has_side_effects=True),
        name="butterfly",
    )
    return call(ranks.T, coefficients, transfer)


def solution(mesh):
    return jax.shard_map(
        per_device,
        mesh=mesh,
        in_specs=(
            P(("grp", "node"), None),
            P(None, ("grp", "node"), None),
            P(None, ("grp", "node")),
        ),
        out_specs=P(("grp", "node"), None),
        check_vma=False,
    )
```

```python
import functools

import jax
import jax.numpy as jnp
from jax import lax
from jax.experimental import pallas as pl
from jax.experimental.pallas import tpu as pltpu
from jax.sharding import PartitionSpec as P

LANES = 128


def split_cols(x):
    high = x.astype(jnp.bfloat16)
    low = (x - high.astype(jnp.float32)).astype(jnp.bfloat16)
    return high, low


def plan(node_bits, group_bits):
    levels, due = [], 0
    for bit in range(node_bits):
        due += 3 if bit else 0
        levels.append(("node", bit, due))
    for bit in range(group_bits):
        due += 2
        levels.append(("grp", bit, due))
    return levels


def kernel(
    levels, ranks_ref, coef_ref, transfer_ref, out_ref,
    raw, mats, own_wide, own, first, landed, mixed, stage,
    raw_sem, stage_sem, first_send, first_recv, send_sem, recv_sem,
):
    depth = coef_ref.shape[0]
    chunks, _, width = first.shape
    pieces, short, _ = landed.shape[1:]
    half = width // 2
    count = len(levels)

    places, partners = [], []
    for axis, bit, _ in levels:
        place = lax.axis_index(axis)
        upper = (place // 2**bit) % 2
        places.append(upper)
        partners.append({axis: place + (1 - 2 * upper) * 2**bit})

    def cols(chunk):
        return pl.ds(pl.multiple_of(chunk * width, width), width)

    def load_chunk(chunk):
        return pltpu.make_async_copy(
            coef_ref.at[:, cols(chunk)], stage.at[chunk], stage_sem.at[chunk]
        )

    def load_matrix(level):
        return pltpu.make_async_copy(transfer_ref.at[level], raw.at[level], raw_sem.at[level])

    def send_first(chunk):
        return pltpu.make_async_remote_copy(
            src_ref=coef_ref.at[:, cols(chunk)],
            dst_ref=first.at[chunk],
            send_sem=first_send.at[chunk],
            recv_sem=first_recv.at[chunk],
            device_id=partners[0],
            device_id_type=pl.DeviceIdType.MESH,
        )

    def send(level, piece):
        return pltpu.make_async_remote_copy(
            src_ref=mixed.at[level - 1, piece],
            dst_ref=landed.at[level - 1, piece],
            send_sem=send_sem.at[level - 1, piece],
            recv_sem=recv_sem.at[level - 1, piece],
            device_id=partners[level],
            device_id_type=pl.DeviceIdType.MESH,
        )

    barrier = pltpu.get_barrier_semaphore()
    for level in range(count):
        pl.semaphore_signal(
            barrier, inc=1, device_id=partners[level], device_id_type=pl.DeviceIdType.MESH
        )
    load_matrix(0).start()
    for chunk in range(chunks):
        load_chunk(chunk).start()
    for level in range(1, count):
        load_matrix(level).start()
    pl.semaphore_wait(barrier, count)
    for chunk in range(chunks):
        send_first(chunk).start()

    left_lanes = lax.broadcasted_iota(jnp.int32, (short, width), 1) < half

    def turn(x):
        return pltpu.roll(x, half, 1)

    def prepare(level):
        load_matrix(level).wait()
        keep = lax.broadcasted_iota(jnp.int32, (depth, depth), 0) < ranks_ref[0, level]
        for side, place in enumerate((places[level], 1 - places[level])):
            block = raw[level, :, pl.ds(pl.multiple_of(place * depth, depth), depth)]
            high, low = split_cols(jnp.where(keep, block, jnp.zeros_like(block)))
            mats[level, :depth, side * depth:(side + 1) * depth] = high
            mats[level, depth:, side * depth:(side + 1) * depth] = low

    def mix(level, mine, other):
        total = jnp.dot(
            mats[level, :, :depth], mine, preferred_element_type=jnp.float32
        ) + jnp.dot(mats[level, :, depth:], other, preferred_element_type=jnp.float32)
        return total[:depth] + total[depth:]

    def spread(top, bottom):
        both = []
        for x in (top, bottom):
            high = x.astype(jnp.bfloat16).astype(jnp.float32)
            both.append(jnp.where(left_lanes, high, x - high).astype(jnp.bfloat16))
        return jnp.concatenate(both, axis=0)

    def spread_packed(packed):
        turned = turn(packed)
        top = jnp.where(left_lanes, packed, turned)
        bottom = jnp.where(left_lanes, turned, packed)
        return spread(top, bottom)

    def task_first(chunk):
        load_chunk(chunk).wait()
        own_wide[...] = jnp.concatenate(split_cols(stage[chunk]), axis=1)
        send_first(chunk).wait_recv()
        total = mix(0, own_wide[...], jnp.concatenate(split_cols(first[chunk]), axis=1))
        result = total[:, :width] + total[:, width:]
        top, bottom = result[:short], result[short:]
        packs = (
            jnp.where(left_lanes, top, turn(bottom)),
            jnp.where(left_lanes, turn(top), bottom),
        )
        for side, packed in enumerate(packs):
            piece = 2 * chunk + side
            mixed[0, piece] = packed
            own[piece] = spread_packed(packed)
            send(1, piece).start()

    def task(level, piece):
        send(level, piece).wait_recv()
        total = mix(level, own[piece], spread_packed(landed[level - 1, piece]))
        result = total + turn(total)
        if level + 1 < count:
            top, bottom = result[:short], result[short:]
            mixed[level, piece] = jnp.where(left_lanes, top, bottom)
            own[piece] = spread(top, bottom)
            send(level + 1, piece).start()
        else:
            here = cols(piece // 2)
            lanes = lax.broadcasted_iota(jnp.int32, (depth, width), 1)
            out_ref[:, here] = jnp.where(lanes < half * (piece % 2), out_ref[:, here], result)

    prepare(0)

    def step(s, carry):
        @pl.when((s % 2 == 0) & (s < pieces))
        def _():
            task_first(s // 2)

        for level, (_, _, due) in enumerate(levels):
            if level:
                @pl.when((s >= due) & (s < due + pieces))
                def _():
                    task(level, s - due)

            if level + 1 < count:
                @pl.when(s == due)
                def _():
                    prepare(level + 1)
        return carry

    lax.fori_loop(0, levels[-1][2] + pieces, step, 0)

    def finish(piece, carry):
        for level in range(1, count):
            send(level, piece).wait_send()
        return carry

    lax.fori_loop(0, pieces, finish, 0)

    def finish_first(chunk, carry):
        send_first(chunk).wait_send()
        return carry

    lax.fori_loop(0, chunks, finish_first, 0)


def per_device(coefficients, transfer, ranks):
    levels = plan(
        lax.axis_size("node").bit_length() - 1, lax.axis_size("grp").bit_length() - 1
    )
    count = len(levels)
    depth, width = coefficients.shape
    chunks = width // LANES
    pieces = 2 * chunks
    short = depth // 2
    call = pl.pallas_call(
        functools.partial(kernel, levels),
        out_shape=jax.ShapeDtypeStruct(coefficients.shape, jnp.float32),
        in_specs=[
            pl.BlockSpec(memory_space=pltpu.SMEM),
            pl.BlockSpec(memory_space=pltpu.HBM),
            pl.BlockSpec(memory_space=pltpu.HBM),
        ],
        out_specs=pl.BlockSpec(memory_space=pltpu.VMEM),
        scratch_shapes=[
            pltpu.VMEM((count, depth, 2 * depth), jnp.float32),
            pltpu.VMEM((count, 2 * depth, 2 * depth), jnp.bfloat16),
            pltpu.VMEM((depth, 2 * LANES), jnp.bfloat16),
            pltpu.VMEM((pieces, depth, LANES), jnp.bfloat16),
            pltpu.VMEM((chunks, depth, LANES), jnp.float32),
            pltpu.VMEM((count - 1, pieces, short, LANES), jnp.float32),
            pltpu.VMEM((count - 1, pieces, short, LANES), jnp.float32),
            pltpu.VMEM((chunks, depth, LANES), jnp.float32),
            pltpu.SemaphoreType.DMA((count,)),
            pltpu.SemaphoreType.DMA((chunks,)),
            pltpu.SemaphoreType.DMA((chunks,)),
            pltpu.SemaphoreType.DMA((chunks,)),
            pltpu.SemaphoreType.DMA((count - 1, pieces)),
            pltpu.SemaphoreType.DMA((count - 1, pieces)),
        ],
        compiler_params=pltpu.CompilerParams(
            collective_id=0, has_side_effects=True, vmem_limit_bytes=55_000_000
        ),
        name="butterfly",
    )
    return call(ranks.T, coefficients, transfer)


def solution(mesh):
    return jax.shard_map(
        per_device,
        mesh=mesh,
        in_specs=(
            P(("grp", "node"), None),
            P(None, ("grp", "node"), None),
            P(None, ("grp", "node")),
        ),
        out_specs=P(("grp", "node"), None),
        check_vma=False,
    )
```

```python
import functools

import jax
import jax.numpy as jnp
from jax import lax
from jax.experimental import pallas as pl
from jax.experimental.pallas import tpu as pltpu
from jax.sharding import PartitionSpec as P

LANES = 128


def split_cols(x):
    high = x.astype(jnp.bfloat16)
    low = (x - high.astype(jnp.float32)).astype(jnp.bfloat16)
    return high, low


def plan(node_bits, group_bits):
    levels, due = [], 0
    for bit in range(node_bits):
        due += (0, 2, 4)[min(bit, 2)]
        levels.append(("node", bit, due))
    for bit in range(group_bits):
        due += 2
        levels.append(("grp", bit, due))
    return levels


def kernel(
    levels, ranks_ref, coef_ref, transfer_ref, out_ref,
    raw, mats, own, first, landed, mixed, stage,
    raw_sem, stage_sem, first_send, first_recv, send_sem, recv_sem,
):
    depth = coef_ref.shape[0]
    chunks, _, width = first.shape
    pieces, short, _ = landed.shape[1:]
    half = width // 2
    count = len(levels)

    places, partners = [], []
    for axis, bit, _ in levels:
        place = lax.axis_index(axis)
        upper = (place // 2**bit) % 2
        places.append(upper)
        partners.append({axis: place + (1 - 2 * upper) * 2**bit})

    def cols(chunk):
        return pl.ds(pl.multiple_of(chunk * width, width), width)

    def load_chunk(chunk):
        return pltpu.make_async_copy(
            coef_ref.at[:, cols(chunk)], stage.at[chunk], stage_sem.at[chunk]
        )

    def load_matrix(level):
        return pltpu.make_async_copy(transfer_ref.at[level], raw.at[level], raw_sem.at[level])

    def send_first(chunk):
        return pltpu.make_async_remote_copy(
            src_ref=coef_ref.at[:, cols(chunk)],
            dst_ref=first.at[chunk],
            send_sem=first_send.at[chunk],
            recv_sem=first_recv.at[chunk],
            device_id=partners[0],
            device_id_type=pl.DeviceIdType.MESH,
        )

    def send(level, piece):
        return pltpu.make_async_remote_copy(
            src_ref=mixed.at[level - 1, piece],
            dst_ref=landed.at[level - 1, piece],
            send_sem=send_sem.at[level - 1, piece],
            recv_sem=recv_sem.at[level - 1, piece],
            device_id=partners[level],
            device_id_type=pl.DeviceIdType.MESH,
        )

    barrier = pltpu.get_barrier_semaphore()
    for level in range(count):
        pl.semaphore_signal(
            barrier, inc=1, device_id=partners[level], device_id_type=pl.DeviceIdType.MESH
        )
    load_matrix(0).start()
    for chunk in range(chunks):
        load_chunk(chunk).start()
    for level in range(1, count):
        load_matrix(level).start()
    pl.semaphore_wait(barrier, count)
    for chunk in range(chunks):
        send_first(chunk).start()

    left_lanes = lax.broadcasted_iota(jnp.int32, (short, width), 1) < half

    def turn(x):
        return pltpu.roll(x, half, 1)

    def prepare(level):
        load_matrix(level).wait()
        keep = lax.broadcasted_iota(jnp.int32, (depth, depth), 0) < ranks_ref[0, level]
        for side, place in enumerate((places[level], 1 - places[level])):
            block = raw[level, :, pl.ds(pl.multiple_of(place * depth, depth), depth)]
            high, low = split_cols(jnp.where(keep, block, jnp.zeros_like(block)))
            mats[level, :depth, side * depth:(side + 1) * depth] = high
            mats[level, depth:, side * depth:(side + 1) * depth] = low

    def fold(total):
        return total[:depth] + total[depth:]

    def mix_own(level, x):
        return fold(jnp.dot(mats[level, :, :depth], x, preferred_element_type=jnp.float32))

    def mix_other(level, x):
        return fold(jnp.dot(mats[level, :, depth:], x, preferred_element_type=jnp.float32))

    def spread(top, bottom):
        both = []
        for x in (top, bottom):
            high = x.astype(jnp.bfloat16).astype(jnp.float32)
            both.append(jnp.where(left_lanes, high, x - high).astype(jnp.bfloat16))
        return jnp.concatenate(both, axis=0)

    def spread_packed(packed):
        turned = turn(packed)
        top = jnp.where(left_lanes, packed, turned)
        bottom = jnp.where(left_lanes, turned, packed)
        return spread(top, bottom)

    def task_first(chunk):
        load_chunk(chunk).wait()
        mine = mix_own(0, jnp.concatenate(split_cols(stage[chunk]), axis=1))
        send_first(chunk).wait_recv()
        total = mine + mix_other(0, jnp.concatenate(split_cols(first[chunk]), axis=1))
        result = total[:, :width] + total[:, width:]
        top, bottom = result[:short], result[short:]
        packs = (
            jnp.where(left_lanes, top, turn(bottom)),
            jnp.where(left_lanes, turn(top), bottom),
        )
        for side, packed in enumerate(packs):
            piece = 2 * chunk + side
            mixed[0, piece] = packed
            own[piece] = spread_packed(packed)
            send(1, piece).start()

    def task(level, piece):
        mine = mix_own(level, own[piece])
        send(level, piece).wait_recv()
        total = mine + mix_other(level, spread_packed(landed[level - 1, piece]))
        result = total + turn(total)
        if level + 1 < count:
            top, bottom = result[:short], result[short:]
            mixed[level, piece] = jnp.where(left_lanes, top, bottom)
            own[piece] = spread(top, bottom)
            send(level + 1, piece).start()
        else:
            here = cols(piece // 2)
            lanes = lax.broadcasted_iota(jnp.int32, (depth, width), 1)
            out_ref[:, here] = jnp.where(lanes < half * (piece % 2), out_ref[:, here], result)

    prepare(0)

    def step(s, carry):
        @pl.when((s % 2 == 0) & (s < pieces))
        def _():
            task_first(s // 2)

        for level, (_, _, due) in enumerate(levels):
            if level:
                @pl.when((s >= due) & (s < due + pieces))
                def _():
                    task(level, s - due)

            if level + 1 < count:
                @pl.when(s == due)
                def _():
                    prepare(level + 1)
        return carry

    lax.fori_loop(0, levels[-1][2] + pieces, step, 0)

    def finish(piece, carry):
        for level in range(1, count):
            send(level, piece).wait_send()
        return carry

    lax.fori_loop(0, pieces, finish, 0)

    def finish_first(chunk, carry):
        send_first(chunk).wait_send()
        return carry

    lax.fori_loop(0, chunks, finish_first, 0)


def per_device(coefficients, transfer, ranks):
    levels = plan(
        lax.axis_size("node").bit_length() - 1, lax.axis_size("grp").bit_length() - 1
    )
    count = len(levels)
    depth, width = coefficients.shape
    chunks = width // LANES
    pieces = 2 * chunks
    short = depth // 2
    call = pl.pallas_call(
        functools.partial(kernel, levels),
        out_shape=jax.ShapeDtypeStruct(coefficients.shape, jnp.float32),
        in_specs=[
            pl.BlockSpec(memory_space=pltpu.SMEM),
            pl.BlockSpec(memory_space=pltpu.HBM),
            pl.BlockSpec(memory_space=pltpu.HBM),
        ],
        out_specs=pl.BlockSpec(memory_space=pltpu.VMEM),
        scratch_shapes=[
            pltpu.VMEM((count, depth, 2 * depth), jnp.float32),
            pltpu.VMEM((count, 2 * depth, 2 * depth), jnp.bfloat16),
            pltpu.VMEM((pieces, depth, LANES), jnp.bfloat16),
            pltpu.VMEM((chunks, depth, LANES), jnp.float32),
            pltpu.VMEM((count - 1, pieces, short, LANES), jnp.float32),
            pltpu.VMEM((count - 1, pieces, short, LANES), jnp.float32),
            pltpu.VMEM((chunks, depth, LANES), jnp.float32),
            pltpu.SemaphoreType.DMA((count,)),
            pltpu.SemaphoreType.DMA((chunks,)),
            pltpu.SemaphoreType.DMA((chunks,)),
            pltpu.SemaphoreType.DMA((chunks,)),
            pltpu.SemaphoreType.DMA((count - 1, pieces)),
            pltpu.SemaphoreType.DMA((count - 1, pieces)),
        ],
        compiler_params=pltpu.CompilerParams(
            collective_id=0, has_side_effects=True, vmem_limit_bytes=55_000_000
        ),
        name="butterfly",
    )
    operands = (ranks.T, coefficients, transfer)
    return call(*(pltpu.with_memory_space_constraint(x, pltpu.HBM) for x in operands))


def solution(mesh):
    return jax.shard_map(
        per_device,
        mesh=mesh,
        in_specs=(
            P(("grp", "node"), None),
            P(None, ("grp", "node"), None),
            P(None, ("grp", "node")),
        ),
        out_specs=P(("grp", "node"), None),
        check_vma=False,
    )
```
